512 devices in a mesh: gx: 4 (over y), gy: 16 (over z_lo, core), ha: 8 (over x, z_hi).
Axes of the slice: x: 4, y: 4, z: 16 (z_hi: 2, z_lo: 8; z = z_hi * 8 + z_lo), core: 2. Of those that a mesh axis runs over, the one named last changes fastest.
Arguments:
- value: float32 [4, 64, 128, 512], P(None, 'ha', 'gy', 'gx'), may hold values from -6 to 6
- obstacles: float32 [5, 128], replicated, may hold values from -1 to 1
- obstacle_slots: int32 [16, 16], P('ha'), may hold values from 0 to 127
- horizon: float32 [1], replicated, may hold values from 0.5 to 2
- speed_offset: int32 [1], replicated, may hold values from 2 to 11
Outputs:
- next_value: float32 [4, 64, 128, 512], P(None, 'ha', 'gy', 'gx')
The draws below stay inside these ranges and needn't reach their ends.
Inputs may be any that keep to these rules, and one draw needn't show every extreme that they name: `obstacle_slots`: each heading group of 4 headings lists 16 obstacle numbers, repeats allowed.
All inputs are finite; a program needn't handle non-finite values.
Results may differ from the reference program's by a relative error of at most 0.00002.
Values sent between devices are 32-bit elements; how exact they have to be, the bound alone decides.
A program may use at most 64 MiB of HBM per device.

```python
import math
import jax
import jax.numpy as jnp
from jax import lax

NV = 4
GH = 4
SLOTS = 16
OBST = 128
NX = 512
NY = 128
NH = 64
GROUPS = 16


def with_ends(array, own_key, least, largest):
    dims = array.shape
    index_at = [jax.random.randint(jax.random.fold_in(own_key, axis), (), 0, dims[axis]) for axis in range(len(dims))]
    array = array.at[tuple(index_at)].set(least)
    longest = dims.index(max(dims))
    index_at[longest] = (index_at[longest] + 1) % dims[longest]
    return array.at[tuple(index_at)].set(largest)


def steps_of(key, dims, cuts, least, top_value):
    level, own = 1.0, jax.random.fold_in(key, 6)
    for axis_at, blocks in cuts:
        draws = jnp.exp(jax.random.uniform(jax.random.fold_in(own, axis_at), (blocks,), jnp.float32, least / len(cuts), top_value / len(cuts)))
        level = level * jnp.repeat(draws, dims[axis_at] // blocks).reshape([-1 if axis == axis_at else 1 for axis in range(len(dims))])
    return level


def scatter_about(own_key, dims, deviation, most, split=(), held_as=jnp.bfloat16):
    level = steps_of(own_key, dims, split, -0.22, 0.18) if split else 1.0
    result = jax.random.normal(own_key, dims, jnp.float32) * deviation * level
    return jnp.minimum(jnp.maximum(result, -most), most).astype(held_as)


def setup_inputs(seed: int = 0) -> dict:
    streams_of = jax.random.split(jax.random.key(seed), 6)
    value = scatter_about(streams_of[0], (NV, NH, NY, NX), 1.0, 6.0, ((1, 8), (2, 16), (3, 4)), jnp.float32)
    obstacles = jnp.clip(jax.random.uniform(streams_of[1], (5, OBST), jnp.float32, -1.0, 1.0), -1.0, 1.0)
    obstacle_slots = with_ends(jax.random.randint(streams_of[2], (GROUPS, SLOTS), 0, OBST), jax.random.fold_in(streams_of[2], 1), 0, OBST - 1).astype(jnp.int32)
    horizon = jnp.clip(jax.random.uniform(streams_of[3], (1,), jnp.float32, 0.5, 2.0), 0.5, 2.0)
    speed_offset = jax.random.randint(streams_of[4], (1,), 2, 12).astype(jnp.int32)
    return {"value": value, "obstacles": obstacles, "obstacle_slots": obstacle_slots, "horizon": horizon, "speed_offset": speed_offset}


cfl_number = 0.75
weno_eps = 1e-06
half_width = 20.0
speed_step = 0.5
turn_limit = 1.0
accel_limit = 4.0
obstacle_speed = 2.0
car_radius = 0.8
body_offsets = (-1.0, 0.0, 1.0)

def weno_side(outer_diff, middle_diff, inner_diff):
    weight_one = 1.0 / 3.0 / jnp.square(weno_eps + jnp.square(middle_diff - outer_diff))
    weight_two = 2.0 / 3.0 / jnp.square(weno_eps + jnp.square(inner_diff - middle_diff))
    return (weight_one * (1.5 * middle_diff - 0.5 * outer_diff) + weight_two * (0.5 * middle_diff + 0.5 * inner_diff)) / (weight_one + weight_two)

def slopes(padded, along_dim, spacing):
    length = padded.shape[along_dim] - 4
    samples = [lax.slice_in_dim(padded, offset_idx, offset_idx + length, axis=along_dim) for offset_idx in range(5)]
    back_far = (samples[1] - samples[0]) / spacing
    back_near = (samples[2] - samples[1]) / spacing
    ahead_near = (samples[3] - samples[2]) / spacing
    ahead_far = (samples[4] - samples[3]) / spacing
    return (weno_side(back_far, back_near, ahead_near), weno_side(ahead_far, ahead_near, back_near))

def hamiltonian_rate(pieces, speeds, angles, spreads, spacings):
    speed_minus, speed_plus = slopes(pieces[0], 0, spacings[0])
    head_minus, head_plus = slopes(pieces[1], 1, spacings[1])
    y_minus, y_plus = slopes(pieces[2], 2, spacings[2])
    x_minus, x_plus = slopes(pieces[3], 3, spacings[3])
    along_x = speeds[:, None, None, None] * jnp.cos(angles)[None, :, None, None]
    along_y = speeds[:, None, None, None] * jnp.sin(angles)[None, :, None, None]
    hamilton = along_x * (0.5 * (x_minus + x_plus)) + along_y * (0.5 * (y_minus + y_plus))
    hamilton = hamilton + turn_limit * jnp.abs(0.5 * (head_minus + head_plus)) + accel_limit * jnp.abs(0.5 * (speed_minus + speed_plus))
    damping = spreads[0] * (x_plus - x_minus) + spreads[1] * (y_plus - y_minus)
    damping = damping + turn_limit * (head_plus - head_minus) + accel_limit * (speed_plus - speed_minus)
    return jnp.minimum(0.0, hamilton - 0.5 * damping)

def speed_bounds(speeds, angles, step_x, step_y):
    along_x = jnp.abs(speeds[:, None] * jnp.cos(angles)[None, :])
    along_y = jnp.abs(speeds[:, None] * jnp.sin(angles)[None, :])
    return (jnp.max(along_x), jnp.max(along_y), jnp.max(along_x / step_x + along_y / step_y))

def group_field(obstacles, horizon, step_time, x_cells, y_cells, angle_group, slot_row):
    moment = horizon[0] + step_time
    centre_x = half_width * obstacles[0] + moment * (obstacle_speed * obstacles[2])
    centre_y = half_width * obstacles[1] + moment * (obstacle_speed * obstacles[3])
    reach = 1.25 + 0.75 * obstacles[4] + car_radius
    centre_x = jnp.take(centre_x, slot_row)[None, :, None, None]
    centre_y = jnp.take(centre_y, slot_row)[None, :, None, None]
    reach = jnp.take(reach, slot_row)[None, :, None, None]
    cosine = jnp.cos(angle_group)[:, None, None, None]
    sine = jnp.sin(angle_group)[:, None, None, None]
    nearest = None
    for offset in body_offsets:
        moved_x = x_cells[None, None, None, :] + offset * cosine
        moved_y = y_cells[None, None, :, None] + offset * sine
        clearance = jnp.sqrt(jnp.square(moved_x - centre_x) + jnp.square(moved_y - centre_y)) - reach
        closest = lax.optimization_barrier(jnp.min(clearance, axis=1))
        nearest = closest if nearest is None else jnp.minimum(nearest, closest)
    return nearest

def advance(surface, time_step, speeds, angles, spreads, spacings):
    pieces = (jnp.pad(surface, ((2, 2), (0, 0), (0, 0), (0, 0)), mode='edge'), jnp.pad(surface, ((0, 0), (2, 2), (0, 0), (0, 0)), mode='wrap'), jnp.pad(surface, ((0, 0), (0, 0), (2, 2), (0, 0)), mode='edge'), jnp.pad(surface, ((0, 0), (0, 0), (0, 0), (2, 2)), mode='edge'))
    return surface + time_step * hamiltonian_rate(pieces, speeds, angles, spreads, spacings)

def reference(value, obstacles, obstacle_slots, horizon, speed_offset):
    step_x = 2.0 * half_width / NX
    step_y = 2.0 * half_width / NY
    step_h = 2.0 * math.pi / NH
    speeds = speed_step * (speed_offset.astype(jnp.float32)[0] + jnp.arange(NV, dtype=jnp.float32))
    angles = jnp.arange(NH, dtype=jnp.int32).astype(jnp.float32) * step_h - math.pi
    spread_x, spread_y, fastest = speed_bounds(speeds, angles, step_x, step_y)
    rate_total = fastest + turn_limit / step_h + accel_limit / speed_step
    time_step = cfl_number / rate_total
    spacings = (speed_step, step_h, step_y, step_x)
    section_one = advance(value, time_step, speeds, angles, (spread_x, spread_y), spacings)
    section_two = advance(section_one, time_step, speeds, angles, (spread_x, spread_y), spacings)
    x_cells = (jnp.arange(NX, dtype=jnp.int32).astype(jnp.float32) + 0.5) * step_x - half_width
    y_cells = (jnp.arange(NY, dtype=jnp.int32).astype(jnp.float32) + 0.5) * step_y - half_width

    def one_group(packed):
        return group_field(obstacles, horizon, time_step, x_cells, y_cells, packed[0], packed[1])
    failure = lax.map(one_group, (angles.reshape(NH // GH, GH), obstacle_slots))
    failure = failure.reshape(NH, NY, NX)
    return jnp.minimum(0.5 * (value + section_two), failure[None])
```

```python
import functools
import math

import jax
import jax.numpy as jnp
import numpy as np
from jax import lax
from jax.experimental import pallas as pl
from jax.experimental.pallas import tpu as pltpu
from jax.sharding import PartitionSpec as P

MESH = pl.DeviceIdType.MESH
f32 = jnp.float32

cfl_number = 0.75
weno_eps = 1e-06
half_width = 20.0
speed_step = 0.5
turn_limit = 1.0
accel_limit = 4.0
obstacle_speed = 2.0
car_radius = 0.8
SLOTS = 16


def grid_tables(heads):
    step = np.float32(2.0 * math.pi / heads)
    angles = np.arange(heads, dtype=np.float32) * step - np.float32(math.pi)
    wide = angles.astype(np.float64)
    return np.cos(wide).astype(np.float32), np.sin(wide).astype(np.float32)


def sides(m2, m1, z0, p1, p2, eps):
    d1, d2, d3, d4 = m1 - m2, z0 - m1, p1 - z0, p2 - p1
    u, v, w = d2 - d1, d3 - d2, d4 - d3
    a, b, c = eps + u * u, eps + v * v, eps + w * w
    a, b, c = a * a, b * b, c * c
    p, q = b + (a + a), b + (c + c)
    r = b / (p * q)
    return p1 - m1, r, (u - v) * q, (w - v) * p


def upwind(parts, ca, cp, cm):
    dm, r, x, y = parts
    return ca * dm + r * (cp * x + cm * y)


def unsigned(parts, coef):
    dm, r, x, y = parts
    hr = 0.5 * r
    return coef * (jnp.abs(dm + hr * (x - y)) + hr * (x + y))


def kernel(
    dims, val_h, obst_h, slots_h, hor_h, off_h, tab_h, out,
    F, G, EX, Q, F1, G1, Q1, fail, obst, slots, hor, off, tab,
    lsem, ha_s, ha_r, y_s, y_r, x_s, x_r, dy_s, dy_r, dx_s, dx_r,
):
    nx, ny, nh, heads, sx, sy, sh, amax_x, amax_y, amax = dims
    gx, gy, ha = lax.axis_index("gx"), lax.axis_index("gy"), lax.axis_index("ha")
    ha_up = (gx, gy, lax.rem(ha + 1, nh))
    ha_dn = (gx, gy, lax.rem(ha + nh - 1, nh))
    y_up, y_dn = (gx, gy + 1, ha), (gx, gy - 1, ha)
    x_up, x_dn = (gx + 1, gy, ha), (gx - 1, gy, ha)
    has_yd, has_yu = gy > 0, gy < ny - 1
    has_xd, has_xu = gx > 0, gx < nx - 1

    bar = pltpu.get_barrier_semaphore()

    def signal(dev):
        pl.semaphore_signal(bar, inc=1, device_id=dev, device_id_type=MESH)

    signal(ha_up)
    signal(ha_dn)
    for cond, dev in ((has_yd, y_dn), (has_yu, y_up), (has_xd, x_dn), (has_xu, x_up)):
        pl.when(cond)(functools.partial(signal, dev))

    loads = [
        pltpu.make_async_copy(src, dst, lsem.at[i])
        for i, (src, dst) in enumerate(
            (
                (off_h, off), (hor_h, hor), (tab_h, tab), (slots_h, slots), (obst_h, obst),
                (val_h, F.at[:, pl.ds(4, 8)]),
            )
        )
    ]
    for load in loads:
        load.start()

    lane = lax.broadcasted_iota(jnp.int32, (8, 128), 1)
    sub = lax.broadcasted_iota(jnp.int32, (8, 128), 0)
    l8 = lane % 8
    low4 = l8 < 4
    grp = lane // 8

    def lroll(x, n):
        return pltpu.roll(x, n % 128, 1)

    def sroll(x, n):
        return pltpu.roll(x, n % 8, 0)

    for load in loads:
        load.wait()

    off0 = off[0]
    offf = off0.astype(f32)
    speeds = [speed_step * (offf + float(k)) for k in range(4)]
    smax = speed_step * jnp.maximum(jnp.abs(offf), jnp.abs(offf + 3.0))
    total = smax * amax + (turn_limit / sh + accel_limit / speed_step)
    dt = cfl_number / total
    spread_x, spread_y = smax * amax_x, smax * amax_y
    moment = hor[0] + dt

    def pack(base, tile_of, idx):
        e = EX[1, idx]
        for s in range(4):
            e = jnp.where(grp == base + s, lroll(tile_of(s), (base + s) * 8 + 4), e)
        EX[1, idx] = e

    def pack_main(h, _):
        pack(0, lambda s: F[s, h + 4], h + 2)
        return 0

    def pack_halo(h, _):
        pack(4, lambda s: G[s, h + 2], h + 2)
        return 0

    lax.fori_loop(0, 8, pack_main, 0)

    xv = ((gx * 128 + lane).astype(f32) + 0.5) * sx - half_width
    yv = ((gy * 8 + sub).astype(f32) + 0.5) * sy - half_width
    for g in range(2):
        cs = [tab[0, ha * 8 + g * 4 + j] for j in range(4)]
        sn = [tab[1, ha * 8 + g * 4 + j] for j in range(4)]

        def one(o, near, g=g, cs=cs, sn=sn):
            k = slots[g, o]
            cx = half_width * obst[0, k] + moment * (obstacle_speed * obst[2, k])
            cy = half_width * obst[1, k] + moment * (obstacle_speed * obst[3, k])
            reach = 1.25 + 0.75 * obst[4, k] + car_radius
            bx, by = xv - cx, yv - cy
            mid = bx * bx + by * by
            new = []
            for j in range(4):
                px, py = bx + cs[j], by + sn[j]
                qx, qy = bx - cs[j], by - sn[j]
                sq = jnp.minimum(mid, jnp.minimum(px * px + py * py, qx * qx + qy * qy))
                new.append(jnp.minimum(near[j], jnp.sqrt(sq) - reach))
            return tuple(new)

        far = jnp.full((8, 128), 3.0e38, f32)
        near = lax.fori_loop(0, SLOTS, one, (far,) * 4)
        for j in range(4):
            fail[g * 4 + j] = near[j]

    count = (
        2
        + jnp.where(has_yd, 1, 0) + jnp.where(has_yu, 1, 0)
        + jnp.where(has_xd, 1, 0) + jnp.where(has_xu, 1, 0)
    )
    pl.semaphore_wait(bar, count)

    def remote(src, dst, s, r, dev):
        return pltpu.make_async_remote_copy(
            src_ref=src, dst_ref=dst, send_sem=s, recv_sem=r, device_id=dev, device_id_type=MESH
        )

    ha_c = []
    for k in range(4):
        up = remote(F.at[:, 11 - k], F.at[:, 3 - k], ha_s.at[0, k], ha_r.at[0, k], ha_up)
        dn = remote(F.at[:, 4 + k], F.at[:, 12 + k], ha_s.at[1, k], ha_r.at[1, k], ha_dn)
        ha_c.append((up, dn))
    for up, dn in ha_c:
        up.start()
        dn.start()

    top, low = pl.ds(4, 4), pl.ds(0, 4)
    mine, near8 = pl.ds(4, 8), pl.ds(2, 8)
    yc_up = remote(F.at[:, mine, top], G.at[:, near8, top], y_s.at[0], y_r.at[0], y_up)
    yc_dn = remote(F.at[:, mine, low], G.at[:, near8, low], y_s.at[1], y_r.at[1], y_dn)
    pl.when(has_yu)(lambda: yc_up.start())
    pl.when(has_yd)(lambda: yc_dn.start())

    def fill_y(h, _):
        @pl.when(jnp.logical_not(has_yd))
        def _():
            for s in range(4):
                row = jnp.broadcast_to(F[s, h + 4, 0:1], (8, 128))
                G[s, h + 2] = jnp.where(sub >= 4, row, G[s, h + 2])

        @pl.when(jnp.logical_not(has_yu))
        def _():
            for s in range(4):
                row = jnp.broadcast_to(F[s, h + 4, 7:8], (8, 128))
                G[s, h + 2] = jnp.where(sub < 4, row, G[s, h + 2])

        return 0

    def fill_x(idx):
        @pl.when(jnp.logical_not(has_xd))
        def _():
            e = EX[1, idx]
            r = lroll(e, -4)
            for j in (1, 2, 3):
                r = jnp.where(l8 == j, lroll(e, j - 4), r)
            EX[0, idx] = r

        @pl.when(jnp.logical_not(has_xu))
        def _():
            e = EX[1, idx]
            r = lroll(e, 1)
            for j in (5, 6, 7):
                r = jnp.where(l8 == j, lroll(e, j - 3), r)
            EX[2, idx] = r

    def make_q(idx):
        left, own, right = EX[0, idx], EX[1, idx], EX[2, idx]
        a = jnp.where(low4, left, own)
        b = jnp.where(low4, own, right)
        Q[idx] = jnp.where(lane < 64, a, lroll(b, 64))

    pl.when(has_yd)(lambda: yc_up.wait_recv())
    pl.when(has_yu)(lambda: yc_dn.wait_recv())
    lax.fori_loop(0, 8, fill_y, 0)
    lax.fori_loop(0, 8, pack_halo, 0)

    xc_up = remote(EX.at[1, near8], EX.at[0, near8], x_s.at[0], x_r.at[0], x_up)
    xc_dn = remote(EX.at[1, near8], EX.at[2, near8], x_s.at[1], x_r.at[1], x_dn)
    pl.when(has_xu)(lambda: xc_up.start())
    pl.when(has_xd)(lambda: xc_dn.start())
    pl.when(has_xd)(lambda: xc_up.wait_recv())
    pl.when(has_xu)(lambda: xc_dn.wait_recv())

    def finish_x(h, _):
        fill_x(h + 2)
        make_q(h + 2)
        return 0

    lax.fori_loop(0, 8, finish_x, 0)

    eps = [weno_eps * s * s for s in (speed_step, sh, sy, sx)]
    k_v, k_h = 0.5 * accel_limit / speed_step, 0.5 * turn_limit / sh

    def coefs(alpha, spread, s):
        return (
            alpha * (0.5 / s), (spread + alpha) * (0.25 / s), (spread - alpha) * (0.25 / s)
        )

    def rate(vs, hs, ys, xs, along_x, along_y):
        acc = unsigned(sides(*vs, eps[0]), k_v) + unsigned(sides(*hs, eps[1]), k_h)
        acc = acc + upwind(sides(*ys, eps[2]), *coefs(along_y, spread_y, sy))
        acc = acc + upwind(sides(*xs, eps[3]), *coefs(along_x, spread_x, sx))
        return dt * jnp.minimum(0.0, acc)

    def y_five(z, other):
        return (
            sroll(jnp.where(sub >= 6, other, z), 2), sroll(jnp.where(sub == 7, other, z), 1), z,
            sroll(jnp.where(sub == 0, other, z), -1), sroll(jnp.where(sub < 2, other, z), -2),
        )

    def x_five(z, other):
        return (
            lroll(jnp.where(lane >= 126, other, z), 2), lroll(jnp.where(lane == 127, other, z), 1), z,
            lroll(jnp.where(lane == 0, other, z), -1), lroll(jnp.where(lane < 2, other, z), -2),
        )

    def clampi(i):
        return min(max(i, 0), 3)

    def turn(h):
        k = lax.rem(ha * 8 + h + heads, heads)
        return tab[0, k], tab[1, k]

    def stage(h, zs, hfive, others, halo, base):
        c, s_ = turn(h)
        res = []
        for s in range(4):
            vs = [zs[clampi(s + j)] for j in (-2, -1, 0, 1, 2)]
            edge = lroll(halo, -((base + s) * 8 + 4))
            res.append(
                zs[s]
                + rate(
                    vs, hfive(s), y_five(zs[s], others[s]), x_five(zs[s], edge),
                    speeds[s] * c, speeds[s] * s_,
                )
            )
        return res

    def one_main(h):
        zs = [F[s, h + 4] for s in range(4)]
        halo = jnp.where(low4, EX[0, h + 2], EX[2, h + 2])
        res = stage(
            h, zs, lambda s: [F[s, h + 4 + j] for j in (-2, -1, 0, 1, 2)],
            [G[s, h + 2] for s in range(4)], halo, 0,
        )
        for s in range(4):
            F1[s, h + 2] = res[s]

    def one_side(h):
        zs = [G[s, h + 2] for s in range(4)]
        halo = jnp.where(low4, EX[0, h + 2], EX[2, h + 2])
        res = stage(
            h, zs, lambda s: [G[s, h + 2 + j] for j in (-2, -1, 0, 1, 2)],
            [F[s, h + 4] for s in range(4)], halo, 4,
        )
        for s in range(4):
            G1[s, h] = res[s]
        z = Q[h + 2]
        s4 = grp % 4
        r8, l8_ = lroll(z, 8), lroll(z, -8)
        vs = (
            jnp.where(s4 == 0, z, jnp.where(s4 == 1, r8, lroll(z, 16))),
            jnp.where(s4 == 0, z, r8),
            z,
            jnp.where(s4 == 3, z, l8_),
            jnp.where(s4 == 3, z, jnp.where(s4 == 2, l8_, lroll(z, -16))),
        )
        swap = jnp.where(grp % 8 < 4, lroll(z, -32), lroll(z, 32))
        xs = (lroll(z, 2), lroll(z, 1), z, lroll(z, -1), lroll(z, -2))
        c, s_ = turn(h)
        sp = speed_step * (offf + s4.astype(f32))
        Q1[h] = z + rate(
            vs, [Q[h + 2 + j] for j in (-2, -1, 0, 1, 2)], y_five(z, swap), xs, sp * c, sp * s_
        )

    def early(i, _):
        one_main(i + 2)
        one_side(i + 2)
        return 0

    lax.fori_loop(0, 4, early, 0)

    pending = []
    for k in range(2):
        for d in range(2):
            ha_c[k][d].wait_recv()
            h = 8 + k if d else -1 - k
            row_up = remote(
                F.at[:, h + 4, top], G.at[:, h + 2, top], dy_s.at[0, d, k], dy_r.at[0, d, k], y_up
            )
            row_dn = remote(
                F.at[:, h + 4, low], G.at[:, h + 2, low], dy_s.at[1, d, k], dy_r.at[1, d, k], y_dn
            )
            pl.when(has_yu)(lambda c=row_up: c.start())
            pl.when(has_yd)(lambda c=row_dn: c.start())
            pack_main(h, 0)
            col_up = remote(
                EX.at[1, h + 2], EX.at[0, h + 2], dx_s.at[0, d, k], dx_r.at[0, d, k], x_up
            )
            col_dn = remote(
                EX.at[1, h + 2], EX.at[2, h + 2], dx_s.at[1, d, k], dx_r.at[1, d, k], x_dn
            )
            pl.when(has_xu)(lambda c=col_up: c.start())
            pl.when(has_xd)(lambda c=col_dn: c.start())
            pending.append((h, row_up, row_dn, col_up, col_dn))

    for h, row_up, row_dn, col_up, col_dn in pending:
        pl.when(has_yd)(lambda c=row_up: c.wait_recv())
        pl.when(has_yu)(lambda c=row_dn: c.wait_recv())
        pl.when(has_xd)(lambda c=col_up: c.wait_recv())
        pl.when(has_xu)(lambda c=col_dn: c.wait_recv())
        fill_y(h, 0)
        fill_x(h + 2)
        make_q(h + 2)

    def late_side(i, _):
        one_side(i + (i // 2) * 4)
        return 0

    lax.fori_loop(0, 4, late_side, 0)

    for k in range(2, 4):
        for d in range(2):
            ha_c[k][d].wait_recv()

    def late_main(i, _):
        one_main(i - 2 + (i // 4) * 4)
        return 0

    lax.fori_loop(0, 8, late_main, 0)

    @pl.when(jnp.logical_not(has_yd))
    def _():
        for h in range(8):
            for s in range(4):
                row = jnp.broadcast_to(F1[s, h + 2, 0:1], (8, 128))
                G1[s, h] = jnp.where(sub >= 4, row, G1[s, h])

    @pl.when(jnp.logical_not(has_yu))
    def _():
        for h in range(8):
            for s in range(4):
                row = jnp.broadcast_to(F1[s, h + 2, 7:8], (8, 128))
                G1[s, h] = jnp.where(sub < 4, row, G1[s, h])

    @pl.when(jnp.logical_not(has_xd))
    def _():
        for h in range(8):
            q = Q1[h]
            r = jnp.where(l8 == 3, lroll(q, -1), jnp.where(l8 == 2, lroll(q, -2), q))
            Q1[h] = jnp.where(lane < 64, r, q)

    @pl.when(jnp.logical_not(has_xu))
    def _():
        for h in range(8):
            q = Q1[h]
            r = jnp.where(l8 == 4, lroll(q, 1), jnp.where(l8 == 5, lroll(q, 2), q))
            Q1[h] = jnp.where(lane < 64, q, r)

    def second(h, _):
        zs = [F1[s, h + 2] for s in range(4)]
        q = Q1[h]
        halo = jnp.where(low4, q, lroll(q, 64))
        res = stage(
            h, zs, lambda s: [F1[s, h + 2 + j] for j in (-2, -1, 0, 1, 2)],
            [G1[s, h] for s in range(4)], halo, 0,
        )
        bound = fail[h]
        for s in range(4):
            out[s, h] = jnp.minimum(0.5 * (F[s, h + 4] + res[s]), bound)
        return 0

    lax.fori_loop(0, 8, second, 0)

    for up, dn in ha_c:
        up.wait_send()
        dn.wait_send()
    pl.when(has_yu)(lambda: yc_up.wait_send())
    pl.when(has_yd)(lambda: yc_dn.wait_send())
    pl.when(has_xu)(lambda: xc_up.wait_send())
    pl.when(has_xd)(lambda: xc_dn.wait_send())
    for h, row_up, row_dn, col_up, col_dn in pending:
        pl.when(has_yu)(lambda c=row_up: c.wait_send())
        pl.when(has_yd)(lambda c=row_dn: c.wait_send())
        pl.when(has_xu)(lambda c=col_up: c.wait_send())
        pl.when(has_xd)(lambda c=col_dn: c.wait_send())


def solution(mesh):
    nx, ny, nh = mesh.shape["gx"], mesh.shape["gy"], mesh.shape["ha"]
    in_specs = (P(None, "ha", "gy", "gx"), P(), P("ha", None), P(), P())
    out_specs = P(None, "ha", "gy", "gx")

    def local(value, obstacles, obstacle_slots, horizon, speed_offset):
        heads = value.shape[1] * nh
        sx = 2.0 * half_width / (value.shape[3] * nx)
        sy = 2.0 * half_width / (value.shape[2] * ny)
        sh = 2.0 * math.pi / heads
        cos, sin = grid_tables(heads)
        c64, s64 = np.abs(cos.astype(np.float64)), np.abs(sin.astype(np.float64))
        dims = (
            nx, ny, nh, heads, sx, sy, sh,
            float(c64.max()), float(s64.max()), float((c64 / sx + s64 / sy).max()),
        )
        anyspec = pl.BlockSpec(memory_space=pl.ANY)
        vm, dma = pltpu.VMEM, pltpu.SemaphoreType.DMA
        return pl.pallas_call(
            functools.partial(kernel, dims),
            out_shape=jax.ShapeDtypeStruct(value.shape, f32),
            in_specs=[anyspec] * 6,
            out_specs=pl.BlockSpec(memory_space=pltpu.VMEM),
            scratch_shapes=[
                vm((4, 16, 8, 128), f32), vm((4, 12, 8, 128), f32), vm((3, 12, 8, 128), f32),
                vm((12, 8, 128), f32), vm((4, 12, 8, 128), f32), vm((4, 8, 8, 128), f32),
                vm((8, 8, 128), f32), vm((8, 8, 128), f32),
                pltpu.SMEM((5, 128), f32), pltpu.SMEM((2, 16), jnp.int32),
                pltpu.SMEM((1,), f32), pltpu.SMEM((1,), jnp.int32), pltpu.SMEM((2, 64), f32),
                dma((6,)), dma((2, 4)), dma((2, 4)), dma((2,)), dma((2,)), dma((2,)), dma((2,)),
                dma((2, 2, 2)), dma((2, 2, 2)), dma((2, 2, 2)), dma((2, 2, 2)),
            ],
            compiler_params=pltpu.CompilerParams(
                collective_id=0, has_side_effects=True, vmem_limit_bytes=16 * 2**20
            ),
            name="tube_step",
        )(value, obstacles, obstacle_slots, horizon, speed_offset, jnp.asarray(np.stack([cos, sin])))

    return jax.shard_map(
        local, mesh=mesh, in_specs=in_specs, out_specs=out_specs, check_vma=False
    )
```

```python
import functools
import math

import jax
import jax.numpy as jnp
import numpy as np
from jax import lax
from jax.experimental import pallas as pl
from jax.experimental.pallas import tpu as pltpu
from jax.sharding import PartitionSpec as P

MESH = pl.DeviceIdType.MESH
f32 = jnp.float32

cfl_number = 0.75
weno_eps = 1e-06
half_width = 20.0
speed_step = 0.5
turn_limit = 1.0
accel_limit = 4.0
obstacle_speed = 2.0
car_radius = 0.8
SLOTS = 16


def grid_tables(heads):
    step = np.float32(2.0 * math.pi / heads)
    angles = np.arange(heads, dtype=np.float32) * step - np.float32(math.pi)
    wide = angles.astype(np.float64)
    return np.cos(wide).astype(np.float32), np.sin(wide).astype(np.float32)


def sides(m2, m1, z0, p1, p2, eps):
    d1, d2, d3, d4 = m1 - m2, z0 - m1, p1 - z0, p2 - p1
    u, v, w = d2 - d1, d3 - d2, d4 - d3
    a, b, c = eps + u * u, eps + v * v, eps + w * w
    a, b, c = a * a, b * b, c * c
    p, q = b + (a + a), b + (c + c)
    r = b / (p * q)
    return p1 - m1, r, (u - v) * q, (w - v) * p


def upwind(parts, ca, cp, cm):
    dm, r, x, y = parts
    return ca * dm + r * (cp * x + cm * y)


def unsigned(parts, coef):
    dm, r, x, y = parts
    hr = 0.5 * r
    return coef * (jnp.abs(dm + hr * (x - y)) + hr * (x + y))


def kernel(
    dims, val_h, obst_h, slots_h, hor_h, off_h, tab_h, out,
    F, G, EX, Q, F1, G1, Q1, fail, obst, slots, hor, off, tab,
    lsem, ha_s, ha_r, y_s, y_r, x_s, x_r, dy_s, dy_r, dx_s, dx_r,
):
    nx, ny, nh, heads, sx, sy, sh, amax_x, amax_y, amax = dims
    gx, gy, ha = lax.axis_index("gx"), lax.axis_index("gy"), lax.axis_index("ha")
    ha_up = (gx, gy, lax.rem(ha + 1, nh))
    ha_dn = (gx, gy, lax.rem(ha + nh - 1, nh))
    y_up, y_dn = (gx, gy + 1, ha), (gx, gy - 1, ha)
    x_up, x_dn = (gx + 1, gy, ha), (gx - 1, gy, ha)
    has_yd, has_yu = gy > 0, gy < ny - 1
    has_xd, has_xu = gx > 0, gx < nx - 1

    bar = pltpu.get_barrier_semaphore()

    def signal(dev):
        pl.semaphore_signal(bar, inc=1, device_id=dev, device_id_type=MESH)

    signal(ha_up)
    signal(ha_dn)
    for cond, dev in ((has_yd, y_dn), (has_yu, y_up), (has_xd, x_dn), (has_xu, x_up)):
        pl.when(cond)(functools.partial(signal, dev))

    loads = [
        pltpu.make_async_copy(src, dst, lsem.at[i])
        for i, (src, dst) in enumerate(
            (
                (off_h, off), (hor_h, hor), (tab_h, tab), (slots_h, slots), (obst_h, obst),
                (val_h, F.at[:, pl.ds(4, 8)]),
            )
        )
    ]
    for load in loads:
        load.start()

    lane = lax.broadcasted_iota(jnp.int32, (8, 128), 1)
    sub = lax.broadcasted_iota(jnp.int32, (8, 128), 0)
    l8 = lane % 8
    low4 = l8 < 4
    grp = lane // 8

    def lroll(x, n):
        return pltpu.roll(x, n % 128, 1)

    def sroll(x, n):
        return pltpu.roll(x, n % 8, 0)

    count = (
        2
        + jnp.where(has_yd, 1, 0) + jnp.where(has_yu, 1, 0)
        + jnp.where(has_xd, 1, 0) + jnp.where(has_xu, 1, 0)
    )
    pl.semaphore_wait(bar, count)

    def remote(src, dst, s, r, dev):
        return pltpu.make_async_remote_copy(
            src_ref=src, dst_ref=dst, send_sem=s, recv_sem=r, device_id=dev, device_id_type=MESH
        )

    top, low = pl.ds(4, 4), pl.ds(0, 4)
    near8 = pl.ds(2, 8)
    yc_up = remote(val_h.at[:, :, top], G.at[:, near8, top], y_s.at[0], y_r.at[0], y_up)
    yc_dn = remote(val_h.at[:, :, low], G.at[:, near8, low], y_s.at[1], y_r.at[1], y_dn)
    pl.when(has_yu)(lambda: yc_up.start())
    pl.when(has_yd)(lambda: yc_dn.start())

    ha_c = []
    for k in range(4):
        up = remote(val_h.at[:, 7 - k], F.at[:, 3 - k], ha_s.at[0, k], ha_r.at[0, k], ha_up)
        dn = remote(val_h.at[:, k], F.at[:, 12 + k], ha_s.at[1, k], ha_r.at[1, k], ha_dn)
        ha_c.append((up, dn))
    for up, dn in ha_c[:2]:
        up.start()
        dn.start()

    for load in loads:
        load.wait()

    off0 = off[0]
    offf = off0.astype(f32)
    speeds = [speed_step * (offf + float(k)) for k in range(4)]
    smax = speed_step * jnp.maximum(jnp.abs(offf), jnp.abs(offf + 3.0))
    total = smax * amax + (turn_limit / sh + accel_limit / speed_step)
    dt = cfl_number / total
    spread_x, spread_y = smax * amax_x, smax * amax_y
    moment = hor[0] + dt

    def pack(base, tile_of, idx):
        e = EX[1, idx]
        for s in range(4):
            e = jnp.where(grp == base + s, lroll(tile_of(s), (base + s) * 8 + 4), e)
        EX[1, idx] = e

    def pack_main(h, _):
        pack(0, lambda s: F[s, h + 4], h + 2)
        return 0

    def pack_halo(h, _):
        pack(4, lambda s: G[s, h + 2], h + 2)
        return 0

    def failure_field():
        xv = ((gx * 128 + lane).astype(f32) + 0.5) * sx - half_width
        yv = ((gy * 8 + sub).astype(f32) + 0.5) * sy - half_width
        for g in range(2):
            cs = [tab[0, ha * 8 + g * 4 + j] for j in range(4)]
            sn = [tab[1, ha * 8 + g * 4 + j] for j in range(4)]

            def one(o, near, g=g, cs=cs, sn=sn):
                k = slots[g, o]
                cx = half_width * obst[0, k] + moment * (obstacle_speed * obst[2, k])
                cy = half_width * obst[1, k] + moment * (obstacle_speed * obst[3, k])
                reach = 1.25 + 0.75 * obst[4, k] + car_radius
                bx, by = xv - cx, yv - cy
                mid = bx * bx + by * by
                new = []
                for j in range(4):
                    px, py = bx + cs[j], by + sn[j]
                    qx, qy = bx - cs[j], by - sn[j]
                    sq = jnp.minimum(mid, jnp.minimum(px * px + py * py, qx * qx + qy * qy))
                    new.append(jnp.minimum(near[j], jnp.sqrt(sq) - reach))
                return tuple(new)

            far = jnp.full((8, 128), 3.0e38, f32)
            near = lax.fori_loop(0, SLOTS, one, (far,) * 4)
            for j in range(4):
                fail[g * 4 + j] = near[j]

    def fill_y(h, _):
        @pl.when(jnp.logical_not(has_yd))
        def _():
            for s in range(4):
                row = jnp.broadcast_to(F[s, h + 4, 0:1], (8, 128))
                G[s, h + 2] = jnp.where(sub >= 4, row, G[s, h + 2])

        @pl.when(jnp.logical_not(has_yu))
        def _():
            for s in range(4):
                row = jnp.broadcast_to(F[s, h + 4, 7:8], (8, 128))
                G[s, h + 2] = jnp.where(sub < 4, row, G[s, h + 2])

        return 0

    def fill_x(idx):
        @pl.when(jnp.logical_not(has_xd))
        def _():
            e = EX[1, idx]
            r = lroll(e, -4)
            for j in (1, 2, 3):
                r = jnp.where(l8 == j, lroll(e, j - 4), r)
            EX[0, idx] = r

        @pl.when(jnp.logical_not(has_xu))
        def _():
            e = EX[1, idx]
            r = lroll(e, 1)
            for j in (5, 6, 7):
                r = jnp.where(l8 == j, lroll(e, j - 3), r)
            EX[2, idx] = r

    def make_q(idx):
        left, own, right = EX[0, idx], EX[1, idx], EX[2, idx]
        a = jnp.where(low4, left, own)
        b = jnp.where(low4, own, right)
        Q[idx] = jnp.where(lane < 64, a, lroll(b, 64))

    lax.fori_loop(0, 8, pack_main, 0)
    pl.when(has_yd)(lambda: yc_up.wait_recv())
    pl.when(has_yu)(lambda: yc_dn.wait_recv())
    for up, dn in ha_c[2:]:
        up.start()
        dn.start()
    lax.fori_loop(0, 8, fill_y, 0)
    lax.fori_loop(0, 8, pack_halo, 0)

    xc_up = remote(EX.at[1, near8], EX.at[0, near8], x_s.at[0], x_r.at[0], x_up)
    xc_dn = remote(EX.at[1, near8], EX.at[2, near8], x_s.at[1], x_r.at[1], x_dn)
    pl.when(has_xu)(lambda: xc_up.start())
    pl.when(has_xd)(lambda: xc_dn.start())
    failure_field()
    pl.when(has_xd)(lambda: xc_up.wait_recv())
    pl.when(has_xu)(lambda: xc_dn.wait_recv())

    def finish_x(h, _):
        fill_x(h + 2)
        make_q(h + 2)
        return 0

    lax.fori_loop(0, 8, finish_x, 0)

    eps = [weno_eps * s * s for s in (speed_step, sh, sy, sx)]
    k_v, k_h = 0.5 * accel_limit / speed_step, 0.5 * turn_limit / sh

    def coefs(alpha, spread, s):
        return (
            alpha * (0.5 / s), (spread + alpha) * (0.25 / s), (spread - alpha) * (0.25 / s)
        )

    def rate(vs, hs, ys, xs, along_x, along_y):
        acc = unsigned(sides(*vs, eps[0]), k_v) + unsigned(sides(*hs, eps[1]), k_h)
        acc = acc + upwind(sides(*ys, eps[2]), *coefs(along_y, spread_y, sy))
        acc = acc + upwind(sides(*xs, eps[3]), *coefs(along_x, spread_x, sx))
        return dt * jnp.minimum(0.0, acc)

    def y_five(z, other):
        return (
            sroll(jnp.where(sub >= 6, other, z), 2), sroll(jnp.where(sub == 7, other, z), 1), z,
            sroll(jnp.where(sub == 0, other, z), -1), sroll(jnp.where(sub < 2, other, z), -2),
        )

    def x_five(z, other):
        return (
            lroll(jnp.where(lane >= 126, other, z), 2), lroll(jnp.where(lane == 127, other, z), 1), z,
            lroll(jnp.where(lane == 0, other, z), -1), lroll(jnp.where(lane < 2, other, z), -2),
        )

    def clampi(i):
        return min(max(i, 0), 3)

    def turn(h):
        k = lax.rem(ha * 8 + h + heads, heads)
        return tab[0, k], tab[1, k]

    def stage(h, zs, hfive, others, halo, base):
        c, s_ = turn(h)
        res = []
        for s in range(4):
            vs = [zs[clampi(s + j)] for j in (-2, -1, 0, 1, 2)]
            edge = lroll(halo, -((base + s) * 8 + 4))
            res.append(
                zs[s]
                + rate(
                    vs, hfive(s), y_five(zs[s], others[s]), x_five(zs[s], edge),
                    speeds[s] * c, speeds[s] * s_,
                )
            )
        return res

    def one_main(h):
        zs = [F[s, h + 4] for s in range(4)]
        halo = jnp.where(low4, EX[0, h + 2], EX[2, h + 2])
        res = stage(
            h, zs, lambda s: [F[s, h + 4 + j] for j in (-2, -1, 0, 1, 2)],
            [G[s, h + 2] for s in range(4)], halo, 0,
        )
        for s in range(4):
            F1[s, h + 2] = res[s]

    def one_side(h):
        zs = [G[s, h + 2] for s in range(4)]
        halo = jnp.where(low4, EX[0, h + 2], EX[2, h + 2])
        res = stage(
            h, zs, lambda s: [G[s, h + 2 + j] for j in (-2, -1, 0, 1, 2)],
            [F[s, h + 4] for s in range(4)], halo, 4,
        )
        for s in range(4):
            G1[s, h] = res[s]
        z = Q[h + 2]
        s4 = grp % 4
        r8, l8_ = lroll(z, 8), lroll(z, -8)
        vs = (
            jnp.where(s4 == 0, z, jnp.where(s4 == 1, r8, lroll(z, 16))),
            jnp.where(s4 == 0, z, r8),
            z,
            jnp.where(s4 == 3, z, l8_),
            jnp.where(s4 == 3, z, jnp.where(s4 == 2, l8_, lroll(z, -16))),
        )
        swap = jnp.where(grp % 8 < 4, lroll(z, -32), lroll(z, 32))
        xs = (lroll(z, 2), lroll(z, 1), z, lroll(z, -1), lroll(z, -2))
        c, s_ = turn(h)
        sp = speed_step * (offf + s4.astype(f32))
        Q1[h] = z + rate(
            vs, [Q[h + 2 + j] for j in (-2, -1, 0, 1, 2)], y_five(z, swap), xs, sp * c, sp * s_
        )

    def fix_edges(h):
        @pl.when(jnp.logical_not(has_yd))
        def _():
            for s in range(4):
                row = jnp.broadcast_to(F1[s, h + 2, 0:1], (8, 128))
                G1[s, h] = jnp.where(sub >= 4, row, G1[s, h])

        @pl.when(jnp.logical_not(has_yu))
        def _():
            for s in range(4):
                row = jnp.broadcast_to(F1[s, h + 2, 7:8], (8, 128))
                G1[s, h] = jnp.where(sub < 4, row, G1[s, h])

        @pl.when(jnp.logical_not(has_xd))
        def _():
            q = Q1[h]
            r = jnp.where(l8 == 3, lroll(q, -1), jnp.where(l8 == 2, lroll(q, -2), q))
            Q1[h] = jnp.where(lane < 64, r, q)

        @pl.when(jnp.logical_not(has_xu))
        def _():
            q = Q1[h]
            r = jnp.where(l8 == 4, lroll(q, 1), jnp.where(l8 == 5, lroll(q, 2), q))
            Q1[h] = jnp.where(lane < 64, q, r)

    def second(h):
        fix_edges(h)
        zs = [F1[s, h + 2] for s in range(4)]
        q = Q1[h]
        halo = jnp.where(low4, q, lroll(q, 64))
        res = stage(
            h, zs, lambda s: [F1[s, h + 2 + j] for j in (-2, -1, 0, 1, 2)],
            [G1[s, h] for s in range(4)], halo, 0,
        )
        bound = fail[h]
        for s in range(4):
            out[s, h] = jnp.minimum(0.5 * (F[s, h + 4] + res[s]), bound)

    def early(i, _):
        one_main(i + 2)
        one_side(i + 2)
        return 0

    lax.fori_loop(0, 4, early, 0)

    pending = []
    for k in range(2):
        for d in range(2):
            ha_c[k][d].wait_recv()
            h = 8 + k if d else -1 - k
            row_up = remote(
                F.at[:, h + 4, top], G.at[:, h + 2, top], dy_s.at[0, d, k], dy_r.at[0, d, k], y_up
            )
            row_dn = remote(
                F.at[:, h + 4, low], G.at[:, h + 2, low], dy_s.at[1, d, k], dy_r.at[1, d, k], y_dn
            )
            pl.when(has_yu)(lambda c=row_up: c.start())
            pl.when(has_yd)(lambda c=row_dn: c.start())
            pack_main(h, 0)
            col_up = remote(
                EX.at[1, h + 2], EX.at[0, h + 2], dx_s.at[0, d, k], dx_r.at[0, d, k], x_up
            )
            col_dn = remote(
                EX.at[1, h + 2], EX.at[2, h + 2], dx_s.at[1, d, k], dx_r.at[1, d, k], x_dn
            )
            pl.when(has_xu)(lambda c=col_up: c.start())
            pl.when(has_xd)(lambda c=col_dn: c.start())
            pending.append((h, row_up, row_dn, col_up, col_dn))

    def inner_main(i, _):
        one_main(i + (i // 2) * 4)
        return 0

    def inner_second(i, _):
        second(i + 2)
        return 0

    lax.fori_loop(0, 4, inner_main, 0)
    lax.fori_loop(0, 4, inner_second, 0)

    for h, row_up, row_dn, col_up, col_dn in pending:
        pl.when(has_yd)(lambda c=row_up: c.wait_recv())
        pl.when(has_yu)(lambda c=row_dn: c.wait_recv())
        pl.when(has_xd)(lambda c=col_up: c.wait_recv())
        pl.when(has_xu)(lambda c=col_dn: c.wait_recv())
        fill_y(h, 0)
        fill_x(h + 2)
        make_q(h + 2)

    def late_side(i, _):
        one_side(i + (i // 2) * 4)
        return 0

    lax.fori_loop(0, 4, late_side, 0)

    for k in range(2, 4):
        for d in range(2):
            ha_c[k][d].wait_recv()

    def late_main(i, _):
        one_main(i - 2 + (i // 2) * 8)
        return 0

    def late_second(i, _):
        second(i + (i // 2) * 4)
        return 0

    lax.fori_loop(0, 4, late_main, 0)
    lax.fori_loop(0, 4, late_second, 0)

    for up, dn in ha_c:
        up.wait_send()
        dn.wait_send()
    pl.when(has_yu)(lambda: yc_up.wait_send())
    pl.when(has_yd)(lambda: yc_dn.wait_send())
    pl.when(has_xu)(lambda: xc_up.wait_send())
    pl.when(has_xd)(lambda: xc_dn.wait_send())
    for h, row_up, row_dn, col_up, col_dn in pending:
        pl.when(has_yu)(lambda c=row_up: c.wait_send())
        pl.when(has_yd)(lambda c=row_dn: c.wait_send())
        pl.when(has_xu)(lambda c=col_up: c.wait_send())
        pl.when(has_xd)(lambda c=col_dn: c.wait_send())


def solution(mesh):
    nx, ny, nh = mesh.shape["gx"], mesh.shape["gy"], mesh.shape["ha"]
    in_specs = (P(None, "ha", "gy", "gx"), P(), P("ha", None), P(), P())
    out_specs = P(None, "ha", "gy", "gx")

    def local(value, obstacles, obstacle_slots, horizon, speed_offset):
        heads = value.shape[1] * nh
        sx = 2.0 * half_width / (value.shape[3] * nx)
        sy = 2.0 * half_width / (value.shape[2] * ny)
        sh = 2.0 * math.pi / heads
        cos, sin = grid_tables(heads)
        c64, s64 = np.abs(cos.astype(np.float64)), np.abs(sin.astype(np.float64))
        dims = (
            nx, ny, nh, heads, sx, sy, sh,
            float(c64.max()), float(s64.max()), float((c64 / sx + s64 / sy).max()),
        )
        anyspec = pl.BlockSpec(memory_space=pltpu.HBM)
        vm, dma = pltpu.VMEM, pltpu.SemaphoreType.DMA
        return pl.pallas_call(
            functools.partial(kernel, dims),
            out_shape=jax.ShapeDtypeStruct(value.shape, f32),
            in_specs=[anyspec] * 3 + [pl.BlockSpec(memory_space=pl.ANY)] * 2 + [anyspec],
            out_specs=pl.BlockSpec(memory_space=pltpu.VMEM),
            scratch_shapes=[
                vm((4, 16, 8, 128), f32), vm((4, 12, 8, 128), f32), vm((3, 12, 8, 128), f32),
                vm((12, 8, 128), f32), vm((4, 12, 8, 128), f32), vm((4, 8, 8, 128), f32),
                vm((8, 8, 128), f32), vm((8, 8, 128), f32),
                pltpu.SMEM((5, 128), f32), pltpu.SMEM((2, 16), jnp.int32),
                pltpu.SMEM((1,), f32), pltpu.SMEM((1,), jnp.int32), pltpu.SMEM((2, 64), f32),
                dma((6,)), dma((2, 4)), dma((2, 4)), dma((2,)), dma((2,)), dma((2,)), dma((2,)),
                dma((2, 2, 2)), dma((2, 2, 2)), dma((2, 2, 2)), dma((2, 2, 2)),
            ],
            compiler_params=pltpu.CompilerParams(
                collective_id=0, has_side_effects=True, vmem_limit_bytes=16 * 2**20
            ),
            name="tube_step",
        )(*(
            x if x.size == 1 else pltpu.with_memory_space_constraint(x, pltpu.HBM)
            for x in (
                value, obstacles, obstacle_slots, horizon, speed_offset,
                jnp.asarray(np.stack([cos, sin])),
            )
        ))

    return jax.shard_map(
        local, mesh=mesh, in_specs=in_specs, out_specs=out_specs, check_vma=False
    )
```

```python
import functools
import math

import jax
import jax.numpy as jnp
import numpy as np
from jax import lax
from jax.experimental import pallas as pl
from jax.experimental.pallas import tpu as pltpu
from jax.sharding import PartitionSpec as P

MESH = pl.DeviceIdType.MESH
f32 = jnp.float32

cfl_number = 0.75
weno_eps = 1e-06
half_width = 20.0
speed_step = 0.5
turn_limit = 1.0
accel_limit = 4.0
obstacle_speed = 2.0
car_radius = 0.8
SLOTS = 16


def grid_tables(heads):
    step = np.float32(2.0 * math.pi / heads)
    angles = np.arange(heads, dtype=np.float32) * step - np.float32(math.pi)
    wide = angles.astype(np.float64)
    return np.cos(wide).astype(np.float32), np.sin(wide).astype(np.float32)


def sides(m2, m1, z0, p1, p2, eps):
    d1, d2, d3, d4 = m1 - m2, z0 - m1, p1 - z0, p2 - p1
    u, v, w = d2 - d1, d3 - d2, d4 - d3
    a, b, c = eps + u * u, eps + v * v, eps + w * w
    a, b, c = a * a, b * b, c * c
    b = 0.5 * b
    p, q = b + a, b + c
    r = b / (p * q)
    return p1 - m1, r, (u - v) * q, (w - v) * p


def upwind(parts, ca, cp, cm):
    dm, r, x, y = parts
    return ca * dm + r * (cp * x + cm * y)


def unsigned(parts, coef):
    dm, r, x, y = parts
    hr = 0.5 * r
    return coef * (jnp.abs(dm + hr * (x - y)) + hr * (x + y))


def kernel(
    dims, val_h, obst_h, slots_h, hor_h, off_h, tab_h, out,
    F, G, EX, Q, F1, G1, Q1, fail, obst, slots, hor, off, tab,
    lsem, ha_s, ha_r, y_s, y_r, x_s, x_r, dy_s, dy_r, dx_s, dx_r,
):
    nx, ny, nh, heads, sx, sy, sh, amax_x, amax_y, amax = dims
    gx, gy, ha = lax.axis_index("gx"), lax.axis_index("gy"), lax.axis_index("ha")
    ha_up = (gx, gy, lax.rem(ha + 1, nh))
    ha_dn = (gx, gy, lax.rem(ha + nh - 1, nh))
    y_up, y_dn = (gx, gy + 1, ha), (gx, gy - 1, ha)
    x_up, x_dn = (gx + 1, gy, ha), (gx - 1, gy, ha)
    has_yd, has_yu = gy > 0, gy < ny - 1
    has_xd, has_xu = gx > 0, gx < nx - 1

    bar = pltpu.get_barrier_semaphore()

    def signal(dev):
        pl.semaphore_signal(bar, inc=1, device_id=dev, device_id_type=MESH)

    signal(ha_up)
    signal(ha_dn)
    for cond, dev in ((has_yd, y_dn), (has_yu, y_up), (has_xd, x_dn), (has_xu, x_up)):
        pl.when(cond)(functools.partial(signal, dev))

    loads = [
        pltpu.make_async_copy(src, dst, lsem.at[i])
        for i, (src, dst) in enumerate(
            (
                (val_h, F.at[:, pl.ds(4, 8)]), (off_h, off), (hor_h, hor), (tab_h, tab),
                (slots_h, slots), (obst_h, obst),
            )
        )
    ]
    for load in loads:
        load.start()

    lane = lax.broadcasted_iota(jnp.int32, (8, 128), 1)
    sub = lax.broadcasted_iota(jnp.int32, (8, 128), 0)
    l8 = lane % 8
    low4 = l8 < 4
    grp = lane // 8

    def lroll(x, n):
        return pltpu.roll(x, n % 128, 1)

    def sroll(x, n):
        return pltpu.roll(x, n % 8, 0)

    count = (
        2
        + jnp.where(has_yd, 1, 0) + jnp.where(has_yu, 1, 0)
        + jnp.where(has_xd, 1, 0) + jnp.where(has_xu, 1, 0)
    )
    loads[0].wait()
    pl.semaphore_wait(bar, count)

    def remote(src, dst, s, r, dev):
        return pltpu.make_async_remote_copy(
            src_ref=src, dst_ref=dst, send_sem=s, recv_sem=r, device_id=dev, device_id_type=MESH
        )

    top, low = pl.ds(4, 4), pl.ds(0, 4)
    mine, near8 = pl.ds(4, 8), pl.ds(2, 8)
    yc_up = remote(F.at[:, mine, top], G.at[:, near8, top], y_s.at[0], y_r.at[0], y_up)
    yc_dn = remote(F.at[:, mine, low], G.at[:, near8, low], y_s.at[1], y_r.at[1], y_dn)
    pl.when(has_yu)(lambda: yc_up.start())
    pl.when(has_yd)(lambda: yc_dn.start())

    ha_c = []
    for k in range(4):
        up = remote(F.at[:, 11 - k], F.at[:, 3 - k], ha_s.at[0, k], ha_r.at[0, k], ha_up)
        dn = remote(F.at[:, 4 + k], F.at[:, 12 + k], ha_s.at[1, k], ha_r.at[1, k], ha_dn)
        ha_c.append((up, dn))
    for up, dn in ha_c[:2]:
        up.start()
        dn.start()

    for load in loads[1:]:
        load.wait()

    off0 = off[0]
    offf = off0.astype(f32)
    speeds = [speed_step * (offf + float(k)) for k in range(4)]
    smax = speed_step * jnp.maximum(jnp.abs(offf), jnp.abs(offf + 3.0))
    total = smax * amax + (turn_limit / sh + accel_limit / speed_step)
    dt = cfl_number / total
    spread_x, spread_y = smax * amax_x, smax * amax_y
    moment = hor[0] + dt

    def pack(base, tile_of, idx):
        e = EX[1, idx]
        for s in range(4):
            e = jnp.where(grp == base + s, lroll(tile_of(s), (base + s) * 8 + 4), e)
        EX[1, idx] = e

    def pack_main(h, _):
        pack(0, lambda s: F[s, h + 4], h + 2)
        return 0

    def pack_halo(h, _):
        pack(4, lambda s: G[s, h + 2], h + 2)
        return 0

    def failure_field():
        xv = ((gx * 128 + lane).astype(f32) + 0.5) * sx - half_width
        yv = ((gy * 8 + sub).astype(f32) + 0.5) * sy - half_width
        for g in range(2):
            cs = [tab[0, ha * 8 + g * 4 + j] for j in range(4)]
            sn = [tab[1, ha * 8 + g * 4 + j] for j in range(4)]

            def one(o, near, g=g, cs=cs, sn=sn):
                k = slots[g, o]
                cx = half_width * obst[0, k] + moment * (obstacle_speed * obst[2, k])
                cy = half_width * obst[1, k] + moment * (obstacle_speed * obst[3, k])
                reach = 1.25 + 0.75 * obst[4, k] + car_radius
                bx, by = xv - cx, yv - cy
                mid = bx * bx + by * by
                new = []
                for j in range(4):
                    px, py = bx + cs[j], by + sn[j]
                    qx, qy = bx - cs[j], by - sn[j]
                    sq = jnp.minimum(mid, jnp.minimum(px * px + py * py, qx * qx + qy * qy))
                    new.append(jnp.minimum(near[j], jnp.sqrt(sq) - reach))
                return tuple(new)

            far = jnp.full((8, 128), 3.0e38, f32)
            near = lax.fori_loop(0, SLOTS, one, (far,) * 4)
            for j in range(4):
                fail[g * 4 + j] = near[j]

    def fill_y(h, _):
        @pl.when(jnp.logical_not(has_yd))
        def _():
            for s in range(4):
                row = jnp.broadcast_to(F[s, h + 4, 0:1], (8, 128))
                G[s, h + 2] = jnp.where(sub >= 4, row, G[s, h + 2])

        @pl.when(jnp.logical_not(has_yu))
        def _():
            for s in range(4):
                row = jnp.broadcast_to(F[s, h + 4, 7:8], (8, 128))
                G[s, h + 2] = jnp.where(sub < 4, row, G[s, h + 2])

        return 0

    def fill_x(idx):
        @pl.when(jnp.logical_not(has_xd))
        def _():
            e = EX[1, idx]
            r = lroll(e, -4)
            for j in (1, 2, 3):
                r = jnp.where(l8 == j, lroll(e, j - 4), r)
            EX[0, idx] = r

        @pl.when(jnp.logical_not(has_xu))
        def _():
            e = EX[1, idx]
            r = lroll(e, 1)
            for j in (5, 6, 7):
                r = jnp.where(l8 == j, lroll(e, j - 3), r)
            EX[2, idx] = r

    def make_q(idx):
        left, own, right = EX[0, idx], EX[1, idx], EX[2, idx]
        a = jnp.where(low4, left, own)
        b = jnp.where(low4, own, right)
        Q[idx] = jnp.where(lane < 64, a, lroll(b, 64))

    lax.fori_loop(0, 8, pack_main, 0)
    pl.when(has_yd)(lambda: yc_up.wait_recv())
    pl.when(has_yu)(lambda: yc_dn.wait_recv())
    for up, dn in ha_c[2:]:
        up.start()
        dn.start()
    lax.fori_loop(0, 8, fill_y, 0)
    lax.fori_loop(0, 8, pack_halo, 0)

    xc_up = remote(EX.at[1, near8], EX.at[0, near8], x_s.at[0], x_r.at[0], x_up)
    xc_dn = remote(EX.at[1, near8], EX.at[2, near8], x_s.at[1], x_r.at[1], x_dn)
    pl.when(has_xu)(lambda: xc_up.start())
    pl.when(has_xd)(lambda: xc_dn.start())
    failure_field()
    pl.when(has_xd)(lambda: xc_up.wait_recv())
    pl.when(has_xu)(lambda: xc_dn.wait_recv())

    def finish_x(h, _):
        fill_x(h + 2)
        make_q(h + 2)
        return 0

    lax.fori_loop(0, 8, finish_x, 0)

    eps = [weno_eps * s * s for s in (speed_step, sh, sy, sx)]
    k_v, k_h = 0.5 * accel_limit / speed_step, 0.5 * turn_limit / sh

    def coefs(alpha, spread, s):
        return (
            alpha * (0.5 / s), (spread + alpha) * (0.25 / s), (spread - alpha) * (0.25 / s)
        )

    def rate(vs, hs, ys, xs, along_x, along_y):
        acc = unsigned(sides(*vs, eps[0]), k_v) + unsigned(sides(*hs, eps[1]), k_h)
        acc = acc + upwind(sides(*ys, eps[2]), *coefs(along_y, spread_y, sy))
        acc = acc + upwind(sides(*xs, eps[3]), *coefs(along_x, spread_x, sx))
        return dt * jnp.minimum(0.0, acc)

    def y_five(z, other):
        return (
            sroll(jnp.where(sub >= 6, other, z), 2), sroll(jnp.where(sub == 7, other, z), 1), z,
            sroll(jnp.where(sub == 0, other, z), -1), sroll(jnp.where(sub < 2, other, z), -2),
        )

    def x_five(z, other):
        return (
            lroll(jnp.where(lane >= 126, other, z), 2), lroll(jnp.where(lane == 127, other, z), 1), z,
            lroll(jnp.where(lane == 0, other, z), -1), lroll(jnp.where(lane < 2, other, z), -2),
        )

    def clampi(i):
        return min(max(i, 0), 3)

    def turn(h):
        k = lax.rem(ha * 8 + h + heads, heads)
        return tab[0, k], tab[1, k]

    def stage(h, zs, hfive, others, halo, base):
        c, s_ = turn(h)
        res = []
        for s in range(4):
            vs = [zs[clampi(s + j)] for j in (-2, -1, 0, 1, 2)]
            edge = lroll(halo, -((base + s) * 8 + 4))
            res.append(
                zs[s]
                + rate(
                    vs, hfive(s), y_five(zs[s], others[s]), x_five(zs[s], edge),
                    speeds[s] * c, speeds[s] * s_,
                )
            )
        return res

    def one_main(h):
        zs = [F[s, h + 4] for s in range(4)]
        halo = jnp.where(low4, EX[0, h + 2], EX[2, h + 2])
        res = stage(
            h, zs, lambda s: [F[s, h + 4 + j] for j in (-2, -1, 0, 1, 2)],
            [G[s, h + 2] for s in range(4)], halo, 0,
        )
        for s in range(4):
            F1[s, h + 2] = res[s]

    def one_side(h):
        zs = [G[s, h + 2] for s in range(4)]
        halo = jnp.where(low4, EX[0, h + 2], EX[2, h + 2])
        res = stage(
            h, zs, lambda s: [G[s, h + 2 + j] for j in (-2, -1, 0, 1, 2)],
            [F[s, h + 4] for s in range(4)], halo, 4,
        )
        for s in range(4):
            G1[s, h] = res[s]
        z = Q[h + 2]
        s4 = grp % 4
        r8, l8_ = lroll(z, 8), lroll(z, -8)
        vs = (
            jnp.where(s4 == 0, z, jnp.where(s4 == 1, r8, lroll(z, 16))),
            jnp.where(s4 == 0, z, r8),
            z,
            jnp.where(s4 == 3, z, l8_),
            jnp.where(s4 == 3, z, jnp.where(s4 == 2, l8_, lroll(z, -16))),
        )
        swap = jnp.where(grp % 8 < 4, lroll(z, -32), lroll(z, 32))
        xs = (lroll(z, 2), lroll(z, 1), z, lroll(z, -1), lroll(z, -2))
        c, s_ = turn(h)
        sp = speed_step * (offf + s4.astype(f32))
        Q1[h] = z + rate(
            vs, [Q[h + 2 + j] for j in (-2, -1, 0, 1, 2)], y_five(z, swap), xs, sp * c, sp * s_
        )

    def fix_edges(h):
        @pl.when(jnp.logical_not(has_yd))
        def _():
            for s in range(4):
                row = jnp.broadcast_to(F1[s, h + 2, 0:1], (8, 128))
                G1[s, h] = jnp.where(sub >= 4, row, G1[s, h])

        @pl.when(jnp.logical_not(has_yu))
        def _():
            for s in range(4):
                row = jnp.broadcast_to(F1[s, h + 2, 7:8], (8, 128))
                G1[s, h] = jnp.where(sub < 4, row, G1[s, h])

        @pl.when(jnp.logical_not(has_xd))
        def _():
            q = Q1[h]
            r = jnp.where(l8 == 3, lroll(q, -1), jnp.where(l8 == 2, lroll(q, -2), q))
            Q1[h] = jnp.where(lane < 64, r, q)

        @pl.when(jnp.logical_not(has_xu))
        def _():
            q = Q1[h]
            r = jnp.where(l8 == 4, lroll(q, 1), jnp.where(l8 == 5, lroll(q, 2), q))
            Q1[h] = jnp.where(lane < 64, q, r)

    def second(h):
        fix_edges(h)
        zs = [F1[s, h + 2] for s in range(4)]
        q = Q1[h]
        halo = jnp.where(low4, q, lroll(q, 64))
        res = stage(
            h, zs, lambda s: [F1[s, h + 2 + j] for j in (-2, -1, 0, 1, 2)],
            [G1[s, h] for s in range(4)], halo, 0,
        )
        bound = fail[h]
        for s in range(4):
            out[s, h] = jnp.minimum(0.5 * (F[s, h + 4] + res[s]), bound)

    def early(i, _):
        one_main(i + 2)
        one_side(i + 2)
        return 0

    lax.fori_loop(0, 4, early, 0)

    pending = []
    for k in range(2):
        for d in range(2):
            ha_c[k][d].wait_recv()
            h = 8 + k if d else -1 - k
            row_up = remote(
                F.at[:, h + 4, pl.ds(6, 2)], G.at[:, h + 2, pl.ds(6, 2)], dy_s.at[0, d, k], dy_r.at[0, d, k], y_up
            )
            row_dn = remote(
                F.at[:, h + 4, pl.ds(0, 2)], G.at[:, h + 2, pl.ds(0, 2)], dy_s.at[1, d, k], dy_r.at[1, d, k], y_dn
            )
            pl.when(has_yu)(lambda c=row_up: c.start())
            pl.when(has_yd)(lambda c=row_dn: c.start())
            pack_main(h, 0)
            col_up = remote(
                EX.at[1, h + 2], EX.at[0, h + 2], dx_s.at[0, d, k], dx_r.at[0, d, k], x_up
            )
            col_dn = remote(
                EX.at[1, h + 2], EX.at[2, h + 2], dx_s.at[1, d, k], dx_r.at[1, d, k], x_dn
            )
            pl.when(has_xu)(lambda c=col_up: c.start())
            pl.when(has_xd)(lambda c=col_dn: c.start())
            pending.append((h, row_up, row_dn, col_up, col_dn))

    def inner_main(i, _):
        one_main(i + (i // 2) * 4)
        return 0

    def inner_second(i, _):
        second(i + 2)
        return 0

    lax.fori_loop(0, 4, inner_main, 0)
    lax.fori_loop(0, 4, inner_second, 0)

    for h, row_up, row_dn, col_up, col_dn in pending:
        pl.when(has_yd)(lambda c=row_up: c.wait_recv())
        pl.when(has_yu)(lambda c=row_dn: c.wait_recv())
        pl.when(has_xd)(lambda c=col_up: c.wait_recv())
        pl.when(has_xu)(lambda c=col_dn: c.wait_recv())
        fill_y(h, 0)
        fill_x(h + 2)
        make_q(h + 2)

    def late_side(i, _):
        one_side(i + (i // 2) * 4)
        return 0

    lax.fori_loop(0, 4, late_side, 0, unroll=4)

    for k in range(2, 4):
        for d in range(2):
            ha_c[k][d].wait_recv()

    def late_main(i, _):
        one_main(i - 2 + (i // 2) * 8)
        return 0

    def late_second(i, _):
        second(i + (i // 2) * 4)
        return 0

    lax.fori_loop(0, 4, late_main, 0, unroll=4)
    lax.fori_loop(0, 4, late_second, 0, unroll=4)

    for up, dn in ha_c:
        up.wait_send()
        dn.wait_send()
    pl.when(has_yu)(lambda: yc_up.wait_send())
    pl.when(has_yd)(lambda: yc_dn.wait_send())
    pl.when(has_xu)(lambda: xc_up.wait_send())
    pl.when(has_xd)(lambda: xc_dn.wait_send())
    for h, row_up, row_dn, col_up, col_dn in pending:
        pl.when(has_yu)(lambda c=row_up: c.wait_send())
        pl.when(has_yd)(lambda c=row_dn: c.wait_send())
        pl.when(has_xu)(lambda c=col_up: c.wait_send())
        pl.when(has_xd)(lambda c=col_dn: c.wait_send())


def solution(mesh):
    nx, ny, nh = mesh.shape["gx"], mesh.shape["gy"], mesh.shape["ha"]
    in_specs = (P(None, "ha", "gy", "gx"), P(), P("ha", None), P(), P())
    out_specs = P(None, "ha", "gy", "gx")

    def local(value, obstacles, obstacle_slots, horizon, speed_offset):
        heads = value.shape[1] * nh
        sx = 2.0 * half_width / (value.shape[3] * nx)
        sy = 2.0 * half_width / (value.shape[2] * ny)
        sh = 2.0 * math.pi / heads
        cos, sin = grid_tables(heads)
        c64, s64 = np.abs(cos.astype(np.float64)), np.abs(sin.astype(np.float64))
        dims = (
            nx, ny, nh, heads, sx, sy, sh,
            float(c64.max()), float(s64.max()), float((c64 / sx + s64 / sy).max()),
        )
        anyspec = pl.BlockSpec(memory_space=pltpu.HBM)
        vm, dma = pltpu.VMEM, pltpu.SemaphoreType.DMA
        return pl.pallas_call(
            functools.partial(kernel, dims),
            out_shape=jax.ShapeDtypeStruct(value.shape, f32),
            in_specs=[anyspec] * 3 + [pl.BlockSpec(memory_space=pl.ANY)] * 2 + [anyspec],
            out_specs=pl.BlockSpec(memory_space=pltpu.VMEM),
            scratch_shapes=[
                vm((4, 16, 8, 128), f32), vm((4, 12, 8, 128), f32), vm((3, 12, 8, 128), f32),
                vm((12, 8, 128), f32), vm((4, 12, 8, 128), f32), vm((4, 8, 8, 128), f32),
                vm((8, 8, 128), f32), vm((8, 8, 128), f32),
                pltpu.SMEM((5, 128), f32), pltpu.SMEM((2, 16), jnp.int32),
                pltpu.SMEM((1,), f32), pltpu.SMEM((1,), jnp.int32), pltpu.SMEM((2, 64), f32),
                dma((6,)), dma((2, 4)), dma((2, 4)), dma((2,)), dma((2,)), dma((2,)), dma((2,)),
                dma((2, 2, 2)), dma((2, 2, 2)), dma((2, 2, 2)), dma((2, 2, 2)),
            ],
            compiler_params=pltpu.CompilerParams(
                collective_id=0, has_side_effects=True, vmem_limit_bytes=16 * 2**20
            ),
            name="tube_step",
        )(*(
            x if x.size == 1 else pltpu.with_memory_space_constraint(x, pltpu.HBM)
            for x in (
                value, obstacles, obstacle_slots, horizon, speed_offset,
                jnp.asarray(np.stack([cos, sin])),
            )
        ))

    return jax.shard_map(
        local, mesh=mesh, in_specs=in_specs, out_specs=out_specs, check_vma=False
    )
```

```python
import functools
import math

import jax
import jax.numpy as jnp
import numpy as np
from jax import lax
from jax.experimental import pallas as pl
from jax.experimental.pallas import tpu as pltpu
from jax.sharding import PartitionSpec as P

MESH = pl.DeviceIdType.MESH
f32 = jnp.float32

cfl_number = 0.75
weno_eps = 1e-06
half_width = 20.0
speed_step = 0.5
turn_limit = 1.0
accel_limit = 4.0
obstacle_speed = 2.0
car_radius = 0.8
SLOTS = 16


def grid_tables(heads):
    step = np.float32(2.0 * math.pi / heads)
    angles = np.arange(heads, dtype=np.float32) * step - np.float32(math.pi)
    wide = angles.astype(np.float64)
    return np.cos(wide).astype(np.float32), np.sin(wide).astype(np.float32)


def sides(m2, m1, z0, p1, p2, eps):
    d1, d2, d3, d4 = m1 - m2, z0 - m1, p1 - z0, p2 - p1
    u, v, w = d2 - d1, d3 - d2, d4 - d3
    a, b, c = eps + u * u, eps + v * v, eps + w * w
    a, b, c = a * a, b * b, c * c
    b = 0.5 * b
    p, q = b + a, b + c
    r = b / (p * q)
    return p1 - m1, r, (u - v) * q, (w - v) * p


def upwind(parts, ca, cp, cm):
    dm, r, x, y = parts
    return ca * dm + r * (cp * x + cm * y)


def unsigned(parts, coef):
    dm, r, x, y = parts
    hr = 0.5 * r
    return coef * (jnp.abs(dm + hr * (x - y)) + hr * (x + y))


def kernel(
    dims, val_h, obst_h, slots_h, hor_h, off_h, tab_h, out,
    F, G, EX, Q, F1, G1, Q1, fail, obst, slots, hor, off, tab,
    lsem, ha_s, ha_r, y_s, y_r, x_s, x_r, dy_s, dy_r, dx_s, dx_r,
):
    nx, ny, nh, heads, sx, sy, sh, amax_x, amax_y, amax = dims
    gx, gy, ha = lax.axis_index("gx"), lax.axis_index("gy"), lax.axis_index("ha")
    ha_up = (gx, gy, lax.rem(ha + 1, nh))
    ha_dn = (gx, gy, lax.rem(ha + nh - 1, nh))
    y_up, y_dn = (gx, gy + 1, ha), (gx, gy - 1, ha)
    x_up, x_dn = (gx + 1, gy, ha), (gx - 1, gy, ha)
    has_yd, has_yu = gy > 0, gy < ny - 1
    has_xd, has_xu = gx > 0, gx < nx - 1

    bar = pltpu.get_barrier_semaphore()

    def signal(dev):
        pl.semaphore_signal(bar, inc=1, device_id=dev, device_id_type=MESH)

    signal(ha_up)
    signal(ha_dn)
    for cond, dev in ((has_yd, y_dn), (has_yu, y_up), (has_xd, x_dn), (has_xu, x_up)):
        pl.when(cond)(functools.partial(signal, dev))

    loads = [
        pltpu.make_async_copy(src, dst, lsem.at[i])
        for i, (src, dst) in enumerate(
            (
                (val_h, F.at[:, pl.ds(4, 8)]), (off_h, off), (hor_h, hor), (tab_h, tab),
                (slots_h, slots), (obst_h, obst),
            )
        )
    ]
    for load in loads:
        load.start()

    lane = lax.broadcasted_iota(jnp.int32, (8, 128), 1)
    sub = lax.broadcasted_iota(jnp.int32, (8, 128), 0)
    l8 = lane % 8
    low4 = l8 < 4
    grp = lane // 8

    def lroll(x, n):
        return pltpu.roll(x, n % 128, 1)

    def sroll(x, n):
        return pltpu.roll(x, n % 8, 0)

    count = (
        2
        + jnp.where(has_yd, 1, 0) + jnp.where(has_yu, 1, 0)
        + jnp.where(has_xd, 1, 0) + jnp.where(has_xu, 1, 0)
    )
    loads[0].wait()
    pl.semaphore_wait(bar, count)

    def remote(src, dst, s, r, dev):
        return pltpu.make_async_remote_copy(
            src_ref=src, dst_ref=dst, send_sem=s, recv_sem=r, device_id=dev, device_id_type=MESH
        )

    top, low = pl.ds(4, 4), pl.ds(0, 4)
    mine, near8 = pl.ds(4, 8), pl.ds(2, 8)
    yc_up = remote(F.at[:, mine, top], G.at[:, near8, top], y_s.at[0], y_r.at[0], y_up)
    yc_dn = remote(F.at[:, mine, low], G.at[:, near8, low], y_s.at[1], y_r.at[1], y_dn)
    pl.when(has_yu)(lambda: yc_up.start())
    pl.when(has_yd)(lambda: yc_dn.start())

    ha_c = []
    for k in range(2):
        up = remote(F.at[:, 11 - k], F.at[:, 3 - k], ha_s.at[0, k], ha_r.at[0, k], ha_up)
        dn = remote(F.at[:, 4 + k], F.at[:, 12 + k], ha_s.at[1, k], ha_r.at[1, k], ha_dn)
        ha_c.append((up, dn))
    up = remote(F.at[:, pl.ds(8, 2)], F.at[:, pl.ds(0, 2)], ha_s.at[0, 2], ha_r.at[0, 2], ha_up)
    dn = remote(F.at[:, pl.ds(6, 2)], F.at[:, pl.ds(14, 2)], ha_s.at[1, 2], ha_r.at[1, 2], ha_dn)
    ha_c.append((up, dn))
    for up, dn in ha_c[:2]:
        up.start()
        dn.start()

    for load in loads[1:]:
        load.wait()

    off0 = off[0]
    offf = off0.astype(f32)
    speeds = [speed_step * (offf + float(k)) for k in range(4)]
    smax = speed_step * jnp.maximum(jnp.abs(offf), jnp.abs(offf + 3.0))
    total = smax * amax + (turn_limit / sh + accel_limit / speed_step)
    dt = cfl_number / total
    spread_x, spread_y = smax * amax_x, smax * amax_y
    moment = hor[0] + dt

    def pack(base, tile_of, idx):
        e = EX[1, idx]
        for s in range(4):
            e = jnp.where(grp == base + s, lroll(tile_of(s), (base + s) * 8 + 4), e)
        EX[1, idx] = e

    def pack_main(h, _):
        pack(0, lambda s: F[s, h + 4], h + 2)
        return 0

    def pack_halo(h, _):
        pack(4, lambda s: G[s, h + 2], h + 2)
        return 0

    def failure_field():
        xv = ((gx * 128 + lane).astype(f32) + 0.5) * sx - half_width
        yv = ((gy * 8 + sub).astype(f32) + 0.5) * sy - half_width
        for g in range(2):
            cs = [tab[0, ha * 8 + g * 4 + j] for j in range(4)]
            sn = [tab[1, ha * 8 + g * 4 + j] for j in range(4)]

            def one(o, near, g=g, cs=cs, sn=sn):
                k = slots[g, o]
                cx = half_width * obst[0, k] + moment * (obstacle_speed * obst[2, k])
                cy = half_width * obst[1, k] + moment * (obstacle_speed * obst[3, k])
                reach = 1.25 + 0.75 * obst[4, k] + car_radius
                bx, by = xv - cx, yv - cy
                mid = bx * bx + by * by
                new = []
                for j in range(4):
                    px, py = bx + cs[j], by + sn[j]
                    qx, qy = bx - cs[j], by - sn[j]
                    sq = jnp.minimum(mid, jnp.minimum(px * px + py * py, qx * qx + qy * qy))
                    new.append(jnp.minimum(near[j], jnp.sqrt(sq) - reach))
                return tuple(new)

            far = jnp.full((8, 128), 3.0e38, f32)
            near = lax.fori_loop(0, SLOTS, one, (far,) * 4)
            for j in range(4):
                fail[g * 4 + j] = near[j]

    def fill_y(h, _):
        @pl.when(jnp.logical_not(has_yd))
        def _():
            for s in range(4):
                row = jnp.broadcast_to(F[s, h + 4, 0:1], (8, 128))
                G[s, h + 2] = jnp.where(sub >= 4, row, G[s, h + 2])

        @pl.when(jnp.logical_not(has_yu))
        def _():
            for s in range(4):
                row = jnp.broadcast_to(F[s, h + 4, 7:8], (8, 128))
                G[s, h + 2] = jnp.where(sub < 4, row, G[s, h + 2])

        return 0

    def fill_x(idx):
        @pl.when(jnp.logical_not(has_xd))
        def _():
            e = EX[1, idx]
            r = lroll(e, -4)
            for j in (1, 2, 3):
                r = jnp.where(l8 == j, lroll(e, j - 4), r)
            EX[0, idx] = r

        @pl.when(jnp.logical_not(has_xu))
        def _():
            e = EX[1, idx]
            r = lroll(e, 1)
            for j in (5, 6, 7):
                r = jnp.where(l8 == j, lroll(e, j - 3), r)
            EX[2, idx] = r

    def make_q(idx):
        left, own, right = EX[0, idx], EX[1, idx], EX[2, idx]
        a = jnp.where(low4, left, own)
        b = jnp.where(low4, own, right)
        Q[idx] = jnp.where(lane < 64, a, lroll(b, 64))

    lax.fori_loop(0, 8, pack_main, 0)
    pl.when(has_yd)(lambda: yc_up.wait_recv())
    pl.when(has_yu)(lambda: yc_dn.wait_recv())
    for up, dn in ha_c[2:]:
        up.start()
        dn.start()
    lax.fori_loop(0, 8, fill_y, 0)
    lax.fori_loop(0, 8, pack_halo, 0)

    xc_up = remote(EX.at[1, near8], EX.at[0, near8], x_s.at[0], x_r.at[0], x_up)
    xc_dn = remote(EX.at[1, near8], EX.at[2, near8], x_s.at[1], x_r.at[1], x_dn)
    pl.when(has_xu)(lambda: xc_up.start())
    pl.when(has_xd)(lambda: xc_dn.start())
    failure_field()
    pl.when(has_xd)(lambda: xc_up.wait_recv())
    pl.when(has_xu)(lambda: xc_dn.wait_recv())

    def finish_x(h, _):
        fill_x(h + 2)
        make_q(h + 2)
        return 0

    lax.fori_loop(0, 8, finish_x, 0)

    eps = [weno_eps * s * s for s in (speed_step, sh, sy, sx)]
    k_v, k_h = 0.5 * accel_limit / speed_step, 0.5 * turn_limit / sh

    def coefs(alpha, spread, s):
        return (
            alpha * (0.5 / s), (spread + alpha) * (0.25 / s), (spread - alpha) * (0.25 / s)
        )

    def rate(vs, hs, ys, xs, along_x, along_y):
        acc = unsigned(sides(*vs, eps[0]), k_v) + unsigned(sides(*hs, eps[1]), k_h)
        acc = acc + upwind(sides(*ys, eps[2]), *coefs(along_y, spread_y, sy))
        acc = acc + upwind(sides(*xs, eps[3]), *coefs(along_x, spread_x, sx))
        return dt * jnp.minimum(0.0, acc)

    def y_five(z, other):
        return (
            sroll(jnp.where(sub >= 6, other, z), 2), sroll(jnp.where(sub == 7, other, z), 1), z,
            sroll(jnp.where(sub == 0, other, z), -1), sroll(jnp.where(sub < 2, other, z), -2),
        )

    def x_five(z, other):
        return (
            lroll(jnp.where(lane >= 126, other, z), 2), lroll(jnp.where(lane == 127, other, z), 1), z,
            lroll(jnp.where(lane == 0, other, z), -1), lroll(jnp.where(lane < 2, other, z), -2),
        )

    def clampi(i):
        return min(max(i, 0), 3)

    def turn(h):
        k = lax.rem(ha * 8 + h + heads, heads)
        return tab[0, k], tab[1, k]

    def stage(h, zs, hfive, others, halo, base):
        c, s_ = turn(h)
        res = []
        for s in range(4):
            vs = [zs[clampi(s + j)] for j in (-2, -1, 0, 1, 2)]
            edge = lroll(halo, -((base + s) * 8 + 4))
            res.append(
                zs[s]
                + rate(
                    vs, hfive(s), y_five(zs[s], others[s]), x_five(zs[s], edge),
                    speeds[s] * c, speeds[s] * s_,
                )
            )
        return res

    def one_main(h):
        zs = [F[s, h + 4] for s in range(4)]
        halo = jnp.where(low4, EX[0, h + 2], EX[2, h + 2])
        res = stage(
            h, zs, lambda s: [F[s, h + 4 + j] for j in (-2, -1, 0, 1, 2)],
            [G[s, h + 2] for s in range(4)], halo, 0,
        )
        for s in range(4):
            F1[s, h + 2] = res[s]

    def one_side(h):
        zs = [G[s, h + 2] for s in range(4)]
        halo = jnp.where(low4, EX[0, h + 2], EX[2, h + 2])
        res = stage(
            h, zs, lambda s: [G[s, h + 2 + j] for j in (-2, -1, 0, 1, 2)],
            [F[s, h + 4] for s in range(4)], halo, 4,
        )
        for s in range(4):
            G1[s, h] = res[s]
        z = Q[h + 2]
        s4 = grp % 4
        r8, l8_ = lroll(z, 8), lroll(z, -8)
        vs = (
            jnp.where(s4 == 0, z, jnp.where(s4 == 1, r8, lroll(z, 16))),
            jnp.where(s4 == 0, z, r8),
            z,
            jnp.where(s4 == 3, z, l8_),
            jnp.where(s4 == 3, z, jnp.where(s4 == 2, l8_, lroll(z, -16))),
        )
        swap = jnp.where(grp % 8 < 4, lroll(z, -32), lroll(z, 32))
        xs = (lroll(z, 2), lroll(z, 1), z, lroll(z, -1), lroll(z, -2))
        c, s_ = turn(h)
        sp = speed_step * (offf + s4.astype(f32))
        Q1[h] = z + rate(
            vs, [Q[h + 2 + j] for j in (-2, -1, 0, 1, 2)], y_five(z, swap), xs, sp * c, sp * s_
        )

    def fix_edges(h):
        @pl.when(jnp.logical_not(has_yd))
        def _():
            for s in range(4):
                row = jnp.broadcast_to(F1[s, h + 2, 0:1], (8, 128))
                G1[s, h] = jnp.where(sub >= 4, row, G1[s, h])

        @pl.when(jnp.logical_not(has_yu))
        def _():
            for s in range(4):
                row = jnp.broadcast_to(F1[s, h + 2, 7:8], (8, 128))
                G1[s, h] = jnp.where(sub < 4, row, G1[s, h])

        @pl.when(jnp.logical_not(has_xd))
        def _():
            q = Q1[h]
            r = jnp.where(l8 == 3, lroll(q, -1), jnp.where(l8 == 2, lroll(q, -2), q))
            Q1[h] = jnp.where(lane < 64, r, q)

        @pl.when(jnp.logical_not(has_xu))
        def _():
            q = Q1[h]
            r = jnp.where(l8 == 4, lroll(q, 1), jnp.where(l8 == 5, lroll(q, 2), q))
            Q1[h] = jnp.where(lane < 64, q, r)

    def second(h):
        fix_edges(h)
        zs = [F1[s, h + 2] for s in range(4)]
        q = Q1[h]
        halo = jnp.where(low4, q, lroll(q, 64))
        res = stage(
            h, zs, lambda s: [F1[s, h + 2 + j] for j in (-2, -1, 0, 1, 2)],
            [G1[s, h] for s in range(4)], halo, 0,
        )
        bound = fail[h]
        for s in range(4):
            out[s, h] = jnp.minimum(0.5 * (F[s, h + 4] + res[s]), bound)

    def early(i, _):
        one_main(i + 2)
        one_side(i + 2)
        return 0

    lax.fori_loop(0, 4, early, 0, unroll=4)

    pending = []
    for k in range(2):
        for d in range(2):
            ha_c[k][d].wait_recv()
            h = 8 + k if d else -1 - k
            row_up = remote(
                F.at[:, h + 4, pl.ds(6, 2)], G.at[:, h + 2, pl.ds(6, 2)], dy_s.at[0, d, k], dy_r.at[0, d, k], y_up
            )
            row_dn = remote(
                F.at[:, h + 4, pl.ds(0, 2)], G.at[:, h + 2, pl.ds(0, 2)], dy_s.at[1, d, k], dy_r.at[1, d, k], y_dn
            )
            pl.when(has_yu)(lambda c=row_up: c.start())
            pl.when(has_yd)(lambda c=row_dn: c.start())
            pack_main(h, 0)
            col_up = remote(
                EX.at[1, h + 2], EX.at[0, h + 2], dx_s.at[0, d, k], dx_r.at[0, d, k], x_up
            )
            col_dn = remote(
                EX.at[1, h + 2], EX.at[2, h + 2], dx_s.at[1, d, k], dx_r.at[1, d, k], x_dn
            )
            pl.when(has_xu)(lambda c=col_up: c.start())
            pl.when(has_xd)(lambda c=col_dn: c.start())
            pending.append((h, row_up, row_dn, col_up, col_dn))

    def inner_main(i, _):
        one_main(i + (i // 2) * 4)
        return 0

    def inner_second(i, _):
        second(i + 2)
        return 0

    lax.fori_loop(0, 4, inner_main, 0, unroll=4)
    lax.fori_loop(0, 4, inner_second, 0, unroll=4)

    for h, row_up, row_dn, col_up, col_dn in pending:
        pl.when(has_yd)(lambda c=row_up: c.wait_recv())
        pl.when(has_yu)(lambda c=row_dn: c.wait_recv())
        pl.when(has_xd)(lambda c=col_up: c.wait_recv())
        pl.when(has_xu)(lambda c=col_dn: c.wait_recv())
        fill_y(h, 0)
        fill_x(h + 2)
        make_q(h + 2)

    def late_side(i, _):
        one_side(i + (i // 2) * 4)
        return 0

    lax.fori_loop(0, 4, late_side, 0, unroll=4)

    for d in range(2):
        ha_c[2][d].wait_recv()

    def late_main(i, _):
        one_main(i - 2 + (i // 2) * 8)
        return 0

    def late_second(i, _):
        second(i + (i // 2) * 4)
        return 0

    lax.fori_loop(0, 4, late_main, 0, unroll=4)
    lax.fori_loop(0, 4, late_second, 0, unroll=4)

    for up, dn in ha_c:
        up.wait_send()
        dn.wait_send()
    pl.when(has_yu)(lambda: yc_up.wait_send())
    pl.when(has_yd)(lambda: yc_dn.wait_send())
    pl.when(has_xu)(lambda: xc_up.wait_send())
    pl.when(has_xd)(lambda: xc_dn.wait_send())
    for h, row_up, row_dn, col_up, col_dn in pending:
        pl.when(has_yu)(lambda c=row_up: c.wait_send())
        pl.when(has_yd)(lambda c=row_dn: c.wait_send())
        pl.when(has_xu)(lambda c=col_up: c.wait_send())
        pl.when(has_xd)(lambda c=col_dn: c.wait_send())


def solution(mesh):
    nx, ny, nh = mesh.shape["gx"], mesh.shape["gy"], mesh.shape["ha"]
    in_specs = (P(None, "ha", "gy", "gx"), P(), P("ha", None), P(), P())
    out_specs = P(None, "ha", "gy", "gx")

    def local(value, obstacles, obstacle_slots, horizon, speed_offset):
        heads = value.shape[1] * nh
        sx = 2.0 * half_width / (value.shape[3] * nx)
        sy = 2.0 * half_width / (value.shape[2] * ny)
        sh = 2.0 * math.pi / heads
        cos, sin = grid_tables(heads)
        c64, s64 = np.abs(cos.astype(np.float64)), np.abs(sin.astype(np.float64))
        dims = (
            nx, ny, nh, heads, sx, sy, sh,
            float(c64.max()), float(s64.max()), float((c64 / sx + s64 / sy).max()),
        )
        anyspec = pl.BlockSpec(memory_space=pltpu.HBM)
        vm, dma = pltpu.VMEM, pltpu.SemaphoreType.DMA
        return pl.pallas_call(
            functools.partial(kernel, dims),
            out_shape=jax.ShapeDtypeStruct(value.shape, f32),
            in_specs=[anyspec] * 3 + [pl.BlockSpec(memory_space=pl.ANY)] * 2 + [anyspec],
            out_specs=pl.BlockSpec(memory_space=pltpu.VMEM),
            scratch_shapes=[
                vm((4, 16, 8, 128), f32), vm((4, 12, 8, 128), f32), vm((3, 12, 8, 128), f32),
                vm((12, 8, 128), f32), vm((4, 12, 8, 128), f32), vm((4, 8, 8, 128), f32),
                vm((8, 8, 128), f32), vm((8, 8, 128), f32),
                pltpu.SMEM((5, 128), f32), pltpu.SMEM((2, 16), jnp.int32),
                pltpu.SMEM((1,), f32), pltpu.SMEM((1,), jnp.int32), pltpu.SMEM((2, 64), f32),
                dma((6,)), dma((2, 4)), dma((2, 4)), dma((2,)), dma((2,)), dma((2,)), dma((2,)),
                dma((2, 2, 2)), dma((2, 2, 2)), dma((2, 2, 2)), dma((2, 2, 2)),
            ],
            compiler_params=pltpu.CompilerParams(
                collective_id=0, has_side_effects=True, vmem_limit_bytes=16 * 2**20
            ),
            name="tube_step",
        )(*(
            x if x.size == 1 else pltpu.with_memory_space_constraint(x, pltpu.HBM)
            for x in (
                value, obstacles, obstacle_slots, horizon, speed_offset,
                jnp.asarray(np.stack([cos, sin])),
            )
        ))

    return jax.shard_map(
        local, mesh=mesh, in_specs=in_specs, out_specs=out_specs, check_vma=False
    )
```
